32 devices in a mesh: coil: 4 (over x, core), slab: 8 (over z, y).
Axes of the slice: x: 2, y: 2, z: 4, core: 2. Of those that a mesh axis runs over, the one named last changes fastest.
Arguments:
- kspace: bfloat16 [2, 8, 2, 32, 384, 128], P(None, 'coil', None, None, 'slab'), may hold values from -6 to 6
- coil_maps: bfloat16 [2, 8, 32, 384, 384], P(None, 'coil', None, 'slab'), may hold values from -1.1953125 to 1.1953125
- line_index: int32 [2, 384, 128], P(None, 'slab'), may hold values from 0 to 383, as said below
Outputs:
- harmonic_image: float32 [32, 2, 384, 384], P('coil', None, 'slab')
The draws below stay inside these ranges and needn't reach their ends.
Inputs may be any that keep to these rules, and one draw needn't show every extreme that they name: `line_index`: for each phase offset and kz plane the 128 ky indices are distinct.
All inputs are finite; a program needn't handle non-finite values.
Results may differ from the reference program's by a relative error of at most 0.0043.
Values may be sent and summed in bfloat16 or wider, within the bound.
A program may use at most 64 MiB of HBM per device.

```python
import math
import jax
import jax.numpy as jnp
from jax import lax

NY = 384
NZ = 384
LINES = 128
OFFS = 2
PHASES = 8
XR = 32
COILS = 8


def pick_row(row_key):
    return jax.random.permutation(row_key, NY)[:LINES]


def draw_line_index(key, part):
    row_keys = jax.random.split(jax.random.fold_in(key, 17), OFFS * NZ)
    chosen = jax.vmap(pick_row)(row_keys)
    return chosen.reshape(OFFS, NZ, LINES).astype(jnp.int32)


def raised(result, rng, source, target, shards_of, factor):
    def block_of(position):
        return (jnp.arange(result.shape[position]) // (result.shape[position] // shards_of)).reshape((-1,) + (1,) * (result.ndim - 1 - position))

    first = jax.random.permutation(rng, shards_of)[block_of(target)]
    second = (block_of(target) + shards_of // 2) % shards_of
    return jnp.where((block_of(source) == first) | (block_of(source) == second), factor * result, result)


def level_of(key, dims, shards, least, top_value):
    level = 1.0
    for axis_at, parts in shards:
        draws = jax.random.uniform(jax.random.fold_in(jax.random.fold_in(key, 6), axis_at), (parts,), jnp.float32, least / len(shards), top_value / len(shards))
        level = level * jnp.repeat(jnp.exp(draws), dims[axis_at] // parts).reshape((-1,) + (1,) * (len(dims) - 1 - axis_at))
    return level


def bell_draw(own_key, dims, scale, most, pieces=(), kind=jnp.bfloat16):
    array = scale * jax.random.normal(own_key, dims, jnp.float32)
    if pieces:
        array = array * level_of(own_key, dims, pieces, -0.22, 0.18)
    return jnp.clip(array, -most, most).astype(kind)


def heavy_noise(rng, shape, width, limit, pieces, heavy, dtype=jnp.bfloat16):
    values = width * jax.random.normal(rng, shape, jnp.float32)
    if pieces:
        values = values * level_of(rng, shape, pieces, -0.22, 0.18)
    return jnp.clip(raised(values, jax.random.fold_in(rng, 3), *heavy), -limit, limit).astype(dtype)


def setup_inputs(seed: int = 0) -> dict:
    arg_keys = jax.random.split(jax.random.key(seed), 4)
    return {
        "kspace": bell_draw(arg_keys[0], (2, COILS, OFFS, XR, NZ, LINES), 1.0, 6.0, ((1, 4), (4, 8))),
        "coil_maps": heavy_noise(arg_keys[1], (2, COILS, XR, NY, NZ), 0.2, 1.1953125, ((1, 4), (3, 8)), (1, 2, 4, 2.0)),
        "line_index": draw_line_index(jax.random.fold_in(arg_keys[3], 71), 0),
    }


def line_tables(line_index, length):
    positions = lax.broadcasted_iota(jnp.int32, (1, 1, 1, length), 3)
    turn_count = line_index[..., None] * positions % length
    angles = turn_count.astype(jnp.float32) * (2.0 * math.pi / length)
    scaling = 1.0 / math.sqrt(length)
    return ((jnp.cos(angles) * scaling).astype(jnp.bfloat16), (jnp.sin(angles) * scaling).astype(jnp.bfloat16))

def dense_tables(length):
    row_pos = lax.broadcasted_iota(jnp.int32, (length, length), 0)
    col_pos = lax.broadcasted_iota(jnp.int32, (length, length), 1)
    turn_count = row_pos * col_pos % length
    angles = turn_count.astype(jnp.float32) * (2.0 * math.pi / length)
    scaling = 1.0 / math.sqrt(length)
    return ((jnp.cos(angles) * scaling).astype(jnp.bfloat16), (jnp.sin(angles) * scaling).astype(jnp.bfloat16))

def fold_offsets(real_part, imag_part, fold_axis):
    sum_real = None
    sum_imag = None
    for offset in range(real_part.shape[fold_axis]):
        phase_angle = 2.0 * math.pi * offset / PHASES
        cosine = math.cos(phase_angle)
        sine = math.sin(phase_angle)
        here_real = jnp.take(real_part, offset, axis=fold_axis)
        here_imag = jnp.take(imag_part, offset, axis=fold_axis)
        term_real = cosine * here_real + sine * here_imag
        term_imag = cosine * here_imag - sine * here_real
        if sum_real is None:
            sum_real, sum_imag = (term_real, term_imag)
        else:
            sum_real, sum_imag = (sum_real + term_real, sum_imag + term_imag)
    return jnp.stack([sum_real, sum_imag]).astype(jnp.bfloat16)

def reference(kspace, coil_maps, line_index):
    line_cos, line_sin = line_tables(line_index, NY)
    line_cos = line_cos.astype(jnp.float32)
    line_sin = line_sin.astype(jnp.float32)
    depth_cos, depth_sin = dense_tables(NZ)
    depth_cos = depth_cos.astype(jnp.float32)
    depth_sin = depth_sin.astype(jnp.float32)
    highest = lax.Precision.HIGHEST

    def one_coil(coil, totals):
        samples = lax.dynamic_index_in_dim(kspace, coil, 1, keepdims=False).astype(jnp.float32)

        def lines_to_rows(left, right):
            return jnp.einsum('txkl,tkly->txyk', left, right, precision=highest)
        hybrid_real = lines_to_rows(samples[0], line_cos) - lines_to_rows(samples[1], line_sin)
        hybrid_imag = lines_to_rows(samples[0], line_sin) + lines_to_rows(samples[1], line_cos)
        folded = fold_offsets(hybrid_real, hybrid_imag, 0).astype(jnp.float32)

        def depth(left, right):
            return jnp.einsum('xyk,kz->xyz', left, right, precision=highest)
        image_real = depth(folded[0], depth_cos) - depth(folded[1], depth_sin)
        image_imag = depth(folded[0], depth_sin) + depth(folded[1], depth_cos)
        maps = lax.dynamic_index_in_dim(coil_maps, coil, 1, keepdims=False).astype(jnp.float32)
        add_real = maps[0] * image_real + maps[1] * image_imag
        add_imag = maps[0] * image_imag - maps[1] * image_real
        return (totals[0] + add_real, totals[1] + add_imag)
    zeros = jnp.zeros((XR, NY, NZ), jnp.float32)
    sum_real, sum_imag = lax.fori_loop(0, COILS, one_coil, (zeros, zeros))
    return jnp.stack([sum_real, sum_imag], axis=1)
```

```python
import functools
import math

import jax
import jax.numpy as jnp
import numpy as np
from jax import lax
from jax.experimental import pallas as pl
from jax.experimental.pallas import tpu as pltpu
from jax.sharding import PartitionSpec as P

PHASES = 8
LANES = 128
MESH = pl.DeviceIdType.MESH


def up(value, unit):
    return -(-value // unit) * unit


def dense_table(rows, row_ok, length):
    turns = rows[:, None].astype(np.int64) * np.arange(length)[None, :] % length
    angles = turns.astype(np.float64) * (2.0 * math.pi / length)
    scaling = row_ok[:, None] / math.sqrt(length)
    cos, sin = np.cos(angles) * scaling, np.sin(angles) * scaling
    return np.concatenate([cos, sin], 1), np.concatenate([-sin, cos], 1)


def kernel(
    dims,
    kspace_ref, maps_ref, index_ref, ky_ref, kz_ref, out_ref,
    raw, samples, grid, maps, send, recv, image, part_send, part_recv,
    in_sem, send_sem, recv_sem, own_sem, psend_sem, precv_sem,
):
    slab, coil, coils, offs, xr, kzb, kzp, lines, ny, yb, nz = dims
    me_s, me_c = lax.axis_index("slab"), lax.axis_index("coil")
    rows = 2 * coils * xr
    kzs = up(kzb, 8)
    chunks = xr // slab
    xo = xr // coil
    owners = slab // xo

    load_k = pltpu.make_async_copy(kspace_ref, raw, in_sem.at[0])
    load_k.start()
    load_m = pltpu.make_async_copy(maps_ref, maps, in_sem.at[1])
    load_m.start()

    barrier = pltpu.get_barrier_semaphore()
    for o in range(1, slab):
        pl.semaphore_signal(
            barrier, inc=1, device_id={"slab": lax.rem(me_s + o, slab)}, device_id_type=MESH
        )
    for o in range(1, coil):
        pl.semaphore_signal(
            barrier, inc=1, device_id={"coil": lax.rem(me_c + o, coil)}, device_id_type=MESH
        )

    if kzp != kzb:
        grid[...] = jnp.zeros_like(grid)
    load_k.wait()

    def unpack(x, carry):
        for c in range(coils):
            for t in range(offs):
                angle = 2.0 * math.pi * t / PHASES
                real = raw[0, c, t, x].astype(jnp.float32)
                imag = raw[1, c, t, x].astype(jnp.float32)
                if t:
                    cosine, sine = math.cos(angle), math.sin(angle)
                    real, imag = cosine * real + sine * imag, cosine * imag - sine * real
                for part, value in ((0, real), (1, imag)):
                    at = pl.multiple_of(((part * coils + c) * xr + x) * kzs, 8)
                    samples[t, pl.ds(at, kzb), :] = value
        return carry

    lax.fori_loop(0, xr, unpack, 0)

    ky_at = lax.broadcasted_iota(jnp.int32, (ny, offs * lines), 0)

    def place(kz, carry):
        picked = jnp.concatenate([index_ref[t, pl.ds(kz, 1), :] for t in range(offs)], axis=1)
        hot = jnp.where(ky_at == picked, 1.0, 0.0).astype(jnp.bfloat16)
        left = jnp.concatenate(
            [samples[t, pl.ds(kz, rows, stride=kzs), :].astype(jnp.bfloat16) for t in range(offs)],
            axis=1,
        )
        grid_at = pl.multiple_of(kz * rows, 8)
        placed = lax.dot_general(
            left, hot, (((1,), (1,)), ((), ())), preferred_element_type=jnp.float32
        )
        for j in range(ny // LANES):
            grid[j, pl.ds(grid_at, rows), :] = placed[:, j * LANES : (j + 1) * LANES]
        return carry

    lax.fori_loop(0, kzb, place, 0)

    pl.semaphore_wait(barrier, slab + coil - 2)

    def chunk_of(k):
        return lax.rem(lax.div(me_c, owners) + 1 + k, chunks)

    def send_copy(k, c, o):
        return pltpu.make_async_remote_copy(
            src_ref=send.at[k, c, lax.rem(me_s + o, slab)],
            dst_ref=recv.at[k, c, me_s],
            send_sem=send_sem.at[k, c, o],
            recv_sem=recv_sem.at[k, c, o],
            device_id={"slab": lax.rem(me_s + o, slab)},
            device_id_type=MESH,
        )

    def recv_copy(k, c, o):
        return pltpu.make_async_remote_copy(
            src_ref=send.at[k, c, lax.rem(me_s + o, slab)],
            dst_ref=recv.at[k, c, lax.rem(me_s + slab - o, slab)],
            send_sem=send_sem.at[k, c, o],
            recv_sem=recv_sem.at[k, c, o],
            device_id={"slab": lax.rem(me_s + o, slab)},
            device_id_type=MESH,
        )

    def own_copy(k, c):
        return pltpu.make_async_copy(send.at[k, c, me_s], recv.at[k, c, me_s], own_sem.at[k, c])

    lane = lax.broadcasted_iota(jnp.int32, (kzp, LANES), 1)

    def rows_pass(step, carry):
        k, c = lax.div(step, coils), lax.rem(step, coils)
        first = chunk_of(k) * slab
        lefts = []
        for i in range(slab):
            pieces = []
            for part in range(2):
                at = (part * coils + c) * xr + first + i
                for j in range(ny // LANES):
                    pieces.append(grid[j, pl.ds(at, kzp, stride=rows), :].astype(jnp.bfloat16))
            lefts.append(jnp.concatenate(pieces, axis=1))
        hybrid = jnp.dot(
            jnp.concatenate(lefts, axis=0), ky_ref[...], preferred_element_type=jnp.float32
        )
        for part in range(2):
            turned = []
            for i in range(slab):
                value = hybrid[i * kzp : (i + 1) * kzp, part * ny : (part + 1) * ny]
                turned.append(pltpu.roll(value, i * yb, 1) if i else value)
            for d in range(slab):
                for j in range(ny // LANES):
                    low, high = j * LANES // yb, ((j + 1) * LANES - 1) // yb
                    cut = slice(j * LANES, (j + 1) * LANES)
                    tile = turned[(low - d) % slab][:, cut]
                    for p in range(low + 1, high + 1):
                        tile = jnp.where(
                            lane >= p * yb - j * LANES, turned[(p - d) % slab][:, cut], tile
                        )
                    send[k, c, d, part, :, cut] = tile.astype(jnp.bfloat16)
        for o in range(1, slab):
            send_copy(k, c, o).start()
        own_copy(k, c).start()
        return carry

    lax.fori_loop(0, chunks * coils, rows_pass, 0)
    load_m.wait()

    def part_copy(k, q):
        owner = chunk_of(k) * owners + q
        return pltpu.make_async_remote_copy(
            src_ref=part_send.at[chunk_of(k), pl.ds(q * xo, xo)],
            dst_ref=part_recv.at[lax.rem(owner - me_c + coil, coil)],
            send_sem=psend_sem.at[k, q],
            recv_sem=precv_sem.at[lax.rem(owner - me_c + coil, coil)],
            device_id={"coil": owner},
            device_id_type=MESH,
        )

    def depth_pass(k, carry):
        first = chunk_of(k) * slab

        def one_coil(c, inner):
            own_copy(k, c).wait()
            for o in range(1, slab):
                recv_copy(k, c, o).wait_recv()
            block = recv[k, c].reshape(slab * 2 * kzp, slab * yb)
            image[c] = lax.dot_general(
                block, kz_ref[...], (((0,), (0,)), ((), ())), preferred_element_type=jnp.float32
            )
            return inner

        lax.fori_loop(0, coils, one_coil, 0)
        for p in range(slab):
            x = lax.rem(p - me_s + slab, slab)
            add_real = add_imag = None
            for c in range(coils):
                real = image[c, p * yb : (p + 1) * yb, :nz]
                imag = image[c, p * yb : (p + 1) * yb, nz:]
                map_real = maps[0, c, first + x].astype(jnp.float32)
                map_imag = maps[1, c, first + x].astype(jnp.float32)
                term_real = map_real * real + map_imag * imag
                term_imag = map_real * imag - map_imag * real
                add_real = term_real if add_real is None else add_real + term_real
                add_imag = term_imag if add_imag is None else add_imag + term_imag
            part_send[chunk_of(k), x, 0] = add_real.astype(jnp.bfloat16)
            part_send[chunk_of(k), x, 1] = add_imag.astype(jnp.bfloat16)
        for q in range(owners):
            @pl.when(chunk_of(k) * owners + q != me_c)
            def _():
                part_copy(k, q).start()
        return carry

    lax.fori_loop(0, chunks, depth_pass, 0)

    for o in range(1, coil):
        pltpu.make_async_remote_copy(
            src_ref=part_recv.at[o],
            dst_ref=part_recv.at[o],
            send_sem=psend_sem.at[0, 0],
            recv_sem=precv_sem.at[o],
            device_id={"coil": lax.rem(me_c + o, coil)},
            device_id_type=MESH,
        ).wait_recv()
    own_chunk, own_at = lax.div(me_c, owners), lax.rem(me_c, owners) * xo

    def total(i, carry):
        value = part_send[own_chunk, own_at + i].astype(jnp.float32)
        for o in range(1, coil):
            value = value + part_recv[o, i].astype(jnp.float32)
        out_ref[i] = value
        return carry

    lax.fori_loop(0, xo, total, 0)

    def drain(k, carry):
        for c in range(coils):
            for o in range(1, slab):
                send_copy(k, c, o).wait_send()
        for q in range(owners):
            @pl.when(chunk_of(k) * owners + q != me_c)
            def _():
                part_copy(k, q).wait_send()
        return carry

    lax.fori_loop(0, chunks, drain, 0)


def local(mesh, kspace, coil_maps, line_index):
    slab, coil = mesh.shape["slab"], mesh.shape["coil"]
    _, coils, offs, xr, kzb, lines = kspace.shape
    yb, nz = coil_maps.shape[3:]
    ny = yb * slab
    kzp = up(kzb, 16)
    dims = (slab, coil, coils, offs, xr, kzb, kzp, lines, ny, yb, nz)
    chunks, xo = xr // slab, xr // coil
    owners = slab // xo
    rows = 2 * coils * xr
    f32, bf16 = jnp.float32, jnp.bfloat16

    ky_table = np.concatenate(dense_table(np.arange(ny), np.ones(ny), ny), 0)
    local_kz = np.arange(kzp)
    per_slab = []
    for s in range(slab):
        per_slab += dense_table(s * kzb + local_kz, (local_kz < kzb) * 1.0, nz)
    kz_table = np.concatenate(per_slab, 0)
    ky_table = jnp.asarray(ky_table.astype(np.float32)).astype(bf16)
    kz_table = jnp.asarray(kz_table.astype(np.float32)).astype(bf16)

    vmem, anywhere = pl.BlockSpec(memory_space=pltpu.VMEM), pl.BlockSpec(memory_space=pl.ANY)
    dma = pltpu.SemaphoreType.DMA
    return pl.pallas_call(
        functools.partial(kernel, dims),
        out_shape=jax.ShapeDtypeStruct((xo, 2, yb, nz), f32),
        in_specs=[anywhere, anywhere, vmem, vmem, vmem],
        out_specs=vmem,
        scratch_shapes=[
            pltpu.VMEM(kspace.shape, bf16),
            pltpu.VMEM((offs, rows * up(kzb, 8), lines), f32),
            pltpu.VMEM((ny // LANES, kzp * rows, LANES), f32),
            pltpu.VMEM(coil_maps.shape, bf16),
            pltpu.VMEM((chunks, coils, slab, 2, kzp, ny), bf16),
            pltpu.VMEM((chunks, coils, slab, 2, kzp, ny), bf16),
            pltpu.VMEM((coils, ny, 2 * nz), f32),
            pltpu.VMEM((chunks, slab, 2, yb, nz), bf16),
            pltpu.VMEM((coil, xo, 2, yb, nz), bf16),
            dma((2,)),
            dma((chunks, coils, slab)),
            dma((chunks, coils, slab)),
            dma((chunks, coils)),
            dma((chunks, owners)),
            dma((coil,)),
        ],
        compiler_params=pltpu.CompilerParams(
            collective_id=0, has_side_effects=True, vmem_limit_bytes=63 * 1024 * 1024
        ),
    )(kspace, coil_maps, line_index, ky_table, kz_table)


def solution(mesh):
    placed = (
        P(None, "coil", None, None, "slab", None),
        P(None, "coil", None, "slab", None),
        P(None, "slab", None),
    )
    return jax.shard_map(
        functools.partial(local, mesh),
        mesh=mesh,
        in_specs=placed,
        out_specs=P("coil", None, "slab", None),
        check_vma=False,
    )
```

```python
import functools
import math

import jax
import jax.numpy as jnp
import numpy as np
from jax import lax
from jax.experimental import pallas as pl
from jax.experimental.pallas import tpu as pltpu
from jax.sharding import PartitionSpec as P

PHASES = 8
LANES = 128
UNROLL = 8
VLIM = 52
ROWS = 16
MESH = pl.DeviceIdType.MESH


def ORDER(slab):
    return range(1, slab)


def up(value, unit):
    return -(-value // unit) * unit


def dense_table(rows, row_ok, length):
    turns = rows[:, None].astype(np.int64) * np.arange(length)[None, :] % length
    angles = turns.astype(np.float64) * (2.0 * math.pi / length)
    scaling = row_ok[:, None] / math.sqrt(length)
    cos, sin = np.cos(angles) * scaling, np.sin(angles) * scaling
    return np.concatenate([cos, sin], 1), np.concatenate([-sin, cos], 1)


def kernel(
    dims,
    kspace_ref, maps_ref, index_ref, ky_ref, kz_ref, out_ref,
    raw, samples, grid, maps, ky_tab, kz_tab, send, recv, image, part_send, part_recv,
    in_sem, send_sem, recv_sem, own_sem, psend_sem, precv_sem,
):
    slab, coil, coils, offs, xr, kzb, kzp, lines, ny, yb, nz = dims
    me_s, me_c = lax.axis_index("slab"), lax.axis_index("coil")
    rows = 2 * coils * slab
    kzs = up(kzb, 8)
    chunks = xr // slab
    xo = xr // coil
    owners = slab // xo
    blocks = kzp // ROWS

    barrier = pltpu.get_barrier_semaphore()
    for o in range(1, slab):
        pl.semaphore_signal(
            barrier, inc=1, device_id={"slab": lax.rem(me_s + o, slab)}, device_id_type=MESH
        )
    for o in range(1, coil):
        pl.semaphore_signal(
            barrier, inc=1, device_id={"coil": lax.rem(me_c + o, coil)}, device_id_type=MESH
        )

    load_k = pltpu.make_async_copy(kspace_ref, raw, in_sem.at[0])
    load_m = pltpu.make_async_copy(maps_ref, maps, in_sem.at[1])
    load_y = pltpu.make_async_copy(ky_ref, ky_tab, in_sem.at[2])
    load_z = pltpu.make_async_copy(kz_ref, kz_tab, in_sem.at[3])
    for load in (load_k, load_y, load_m, load_z):
        load.start()

    if kzp != kzb:
        grid[...] = jnp.zeros_like(grid)

    def unpack(first, i, carry):
        for c in range(coils):
            for t in range(offs):
                angle = 2.0 * math.pi * t / PHASES
                real = raw[0, c, t, first + i].astype(jnp.float32)
                imag = raw[1, c, t, first + i].astype(jnp.float32)
                if t:
                    cosine, sine = math.cos(angle), math.sin(angle)
                    real, imag = cosine * real + sine * imag, cosine * imag - sine * real
                for part, value in ((0, real), (1, imag)):
                    at = pl.multiple_of(((part * coils + c) * slab + i) * kzs, 8)
                    samples[t, pl.ds(at, kzb), :] = value
        return carry

    ky_at = lax.broadcasted_iota(jnp.int32, (ny, offs * lines), 0)

    def place(first_kz, step, carry):
        kz = first_kz + step
        picked = jnp.concatenate([index_ref[t, pl.ds(kz, 1), :] for t in range(offs)], axis=1)
        hot = jnp.where(ky_at == picked, 1.0, 0.0).astype(jnp.bfloat16)
        left = jnp.concatenate(
            [samples[t, pl.ds(kz, rows, stride=kzs), :].astype(jnp.bfloat16) for t in range(offs)],
            axis=1,
        )
        grid_at = pl.multiple_of(kz * rows, 8)
        placed = lax.dot_general(
            left, hot, (((1,), (1,)), ((), ())), preferred_element_type=jnp.float32
        )
        for j in range(ny // LANES):
            grid[j, pl.ds(grid_at, rows), :] = placed[:, j * LANES : (j + 1) * LANES]
        return carry


    def chunk_of(k):
        return lax.rem(lax.div(me_c, owners) + 1 + k, chunks)

    def block_copy(k, c, o, kz_at):
        return pltpu.make_async_remote_copy(
            src_ref=send.at[k, c, lax.rem(me_s + o, slab), :, pl.ds(kz_at, ROWS)],
            dst_ref=recv.at[k, c, me_s, :, pl.ds(kz_at, ROWS)],
            send_sem=send_sem.at[k, c, o],
            recv_sem=recv_sem.at[k, c, o],
            device_id={"slab": lax.rem(me_s + o, slab)},
            device_id_type=MESH,
        )

    def send_copy(k, c, o):
        return pltpu.make_async_remote_copy(
            src_ref=send.at[k, c, lax.rem(me_s + o, slab)],
            dst_ref=recv.at[k, c, me_s],
            send_sem=send_sem.at[k, c, o],
            recv_sem=recv_sem.at[k, c, o],
            device_id={"slab": lax.rem(me_s + o, slab)},
            device_id_type=MESH,
        )

    def recv_copy(k, c, o):
        return pltpu.make_async_remote_copy(
            src_ref=send.at[k, c, lax.rem(me_s + o, slab)],
            dst_ref=recv.at[k, c, lax.rem(me_s + slab - o, slab)],
            send_sem=send_sem.at[k, c, o],
            recv_sem=recv_sem.at[k, c, o],
            device_id={"slab": lax.rem(me_s + o, slab)},
            device_id_type=MESH,
        )

    def own_copy(k, c):
        return pltpu.make_async_copy(send.at[k, c, me_s], recv.at[k, c, me_s], own_sem.at[k, c])

    lane = lax.broadcasted_iota(jnp.int32, (ROWS, LANES), 1)

    def rows_pass(k, b, c, carry):
        kz_at = pl.multiple_of(b * ROWS, ROWS)
        lefts = []
        for i in range(slab):
            pieces = []
            for part in range(2):
                at = (part * coils + c) * slab + i
                for j in range(ny // LANES):
                    here = grid[j, pl.ds(kz_at * rows + at, ROWS, stride=rows), :]
                    pieces.append(here.astype(jnp.bfloat16))
            lefts.append(jnp.concatenate(pieces, axis=1))
        hybrid = jnp.dot(
            jnp.concatenate(lefts, axis=0), ky_tab[...], preferred_element_type=jnp.float32
        )
        for part in range(2):
            turned = []
            for i in range(slab):
                value = hybrid[i * ROWS : (i + 1) * ROWS, part * ny : (part + 1) * ny]
                turned.append(pltpu.roll(value, i * yb, 1) if i else value)
            for d in range(slab):
                for j in range(ny // LANES):
                    low, high = j * LANES // yb, ((j + 1) * LANES - 1) // yb
                    cut = slice(j * LANES, (j + 1) * LANES)
                    tile = turned[(low - d) % slab][:, cut]
                    for p in range(low + 1, high + 1):
                        tile = jnp.where(
                            lane >= p * yb - j * LANES, turned[(p - d) % slab][:, cut], tile
                        )
                    send[k, c, d, part, pl.ds(kz_at, ROWS), cut] = tile.astype(jnp.bfloat16)
        for o in ORDER(slab):
            block_copy(k, c, o, kz_at).start()

        @pl.when(b == blocks - 1)
        def _():
            own_copy(k, c).start()

        return carry

    def chunk_pass(k, carry):
        first = chunk_of(k) * slab
        lax.fori_loop(0, slab, functools.partial(unpack, first), 0)

        def block_pass(b, inner):
            count = min(ROWS, kzb)
            lax.fori_loop(0, count, functools.partial(place, b * ROWS), 0, unroll=UNROLL)
            return lax.fori_loop(0, coils, functools.partial(rows_pass, k, b), inner)

        return lax.fori_loop(0, blocks, block_pass, carry)

    load_k.wait()
    load_y.wait()
    pl.semaphore_wait(barrier, slab + coil - 2)
    lax.fori_loop(0, chunks, chunk_pass, 0)
    load_m.wait()
    load_z.wait()

    def part_copy(k, q):
        owner = chunk_of(k) * owners + q
        return pltpu.make_async_remote_copy(
            src_ref=part_send.at[chunk_of(k), pl.ds(q * xo, xo)],
            dst_ref=part_recv.at[lax.rem(owner - me_c + coil, coil)],
            send_sem=psend_sem.at[k, q],
            recv_sem=precv_sem.at[lax.rem(owner - me_c + coil, coil)],
            device_id={"coil": owner},
            device_id_type=MESH,
        )

    def depth_pass(k, carry):
        first = chunk_of(k) * slab

        def one_coil(c, inner):
            own_copy(k, c).wait()
            for o in range(1, slab):
                recv_copy(k, c, o).wait_recv()
            block = recv[k, c].reshape(slab * 2 * kzp, slab * yb)
            image[c] = lax.dot_general(
                block, kz_tab[...], (((0,), (0,)), ((), ())), preferred_element_type=jnp.float32
            )
            return inner

        lax.fori_loop(0, coils, one_coil, 0)
        for p in range(slab):
            x = lax.rem(p - me_s + slab, slab)
            add_real = add_imag = None
            for c in range(coils):
                real = image[c, p * yb : (p + 1) * yb, :nz]
                imag = image[c, p * yb : (p + 1) * yb, nz:]
                map_real = maps[0, c, first + x].astype(jnp.float32)
                map_imag = maps[1, c, first + x].astype(jnp.float32)
                term_real = map_real * real + map_imag * imag
                term_imag = map_real * imag - map_imag * real
                add_real = term_real if add_real is None else add_real + term_real
                add_imag = term_imag if add_imag is None else add_imag + term_imag
            part_send[chunk_of(k), x, 0] = add_real.astype(jnp.bfloat16)
            part_send[chunk_of(k), x, 1] = add_imag.astype(jnp.bfloat16)
        for q in range(owners):
            @pl.when(chunk_of(k) * owners + q != me_c)
            def _():
                part_copy(k, q).start()
        return carry

    lax.fori_loop(0, chunks, depth_pass, 0)

    for o in range(1, coil):
        pltpu.make_async_remote_copy(
            src_ref=part_recv.at[o],
            dst_ref=part_recv.at[o],
            send_sem=psend_sem.at[0, 0],
            recv_sem=precv_sem.at[o],
            device_id={"coil": lax.rem(me_c + o, coil)},
            device_id_type=MESH,
        ).wait_recv()
    own_chunk, own_at = lax.div(me_c, owners), lax.rem(me_c, owners) * xo

    def total(i, carry):
        value = part_send[own_chunk, own_at + i].astype(jnp.float32)
        for o in range(1, coil):
            value = value + part_recv[o, i].astype(jnp.float32)
        out_ref[i] = value
        return carry

    lax.fori_loop(0, xo, total, 0)

    def drain(k, carry):
        for c in range(coils):
            for o in range(1, slab):
                send_copy(k, c, o).wait_send()
        for q in range(owners):
            @pl.when(chunk_of(k) * owners + q != me_c)
            def _():
                part_copy(k, q).wait_send()
        return carry

    lax.fori_loop(0, chunks, drain, 0)


def local(mesh, kspace, coil_maps, line_index):
    slab, coil = mesh.shape["slab"], mesh.shape["coil"]
    _, coils, offs, xr, kzb, lines = kspace.shape
    yb, nz = coil_maps.shape[3:]
    ny = yb * slab
    kzp = up(kzb, 16)
    dims = (slab, coil, coils, offs, xr, kzb, kzp, lines, ny, yb, nz)
    chunks, xo = xr // slab, xr // coil
    owners = slab // xo
    rows = 2 * coils * slab
    f32, bf16 = jnp.float32, jnp.bfloat16

    ky_table = np.concatenate(dense_table(np.arange(ny), np.ones(ny), ny), 0)
    local_kz = np.arange(kzp)
    per_slab = []
    for s in range(slab):
        per_slab += dense_table(s * kzb + local_kz, (local_kz < kzb) * 1.0, nz)
    kz_table = np.concatenate(per_slab, 0)
    ky_table = jnp.asarray(ky_table.astype(np.float32)).astype(bf16)
    kz_table = jnp.asarray(kz_table.astype(np.float32)).astype(bf16)

    vmem, hbm = pl.BlockSpec(memory_space=pltpu.VMEM), pl.BlockSpec(memory_space=pltpu.HBM)
    dma = pltpu.SemaphoreType.DMA
    return pl.pallas_call(
        functools.partial(kernel, dims),
        out_shape=jax.ShapeDtypeStruct((xo, 2, yb, nz), f32),
        in_specs=[hbm, hbm, vmem, hbm, hbm],
        out_specs=vmem,
        scratch_shapes=[
            pltpu.VMEM(kspace.shape, bf16),
            pltpu.VMEM((offs, rows * up(kzb, 8), lines), f32),
            pltpu.VMEM((ny // LANES, kzp * rows, LANES), f32),
            pltpu.VMEM(coil_maps.shape, bf16),
            pltpu.VMEM(ky_table.shape, bf16),
            pltpu.VMEM(kz_table.shape, bf16),
            pltpu.VMEM((chunks, coils, slab, 2, kzp, ny), bf16),
            pltpu.VMEM((chunks, coils, slab, 2, kzp, ny), bf16),
            pltpu.VMEM((coils, ny, 2 * nz), f32),
            pltpu.VMEM((chunks, slab, 2, yb, nz), bf16),
            pltpu.VMEM((coil, xo, 2, yb, nz), bf16),
            dma((4,)),
            dma((chunks, coils, slab)),
            dma((chunks, coils, slab)),
            dma((chunks, coils)),
            dma((chunks, owners)),
            dma((coil,)),
        ],
        compiler_params=pltpu.CompilerParams(
            collective_id=0, has_side_effects=True, vmem_limit_bytes=VLIM * 1024 * 1024
        ),
    )(kspace, coil_maps, line_index, ky_table, kz_table)


def solution(mesh):
    placed = (
        P(None, "coil", None, None, "slab", None),
        P(None, "coil", None, "slab", None),
        P(None, "slab", None),
    )
    return jax.shard_map(
        functools.partial(local, mesh),
        mesh=mesh,
        in_specs=placed,
        out_specs=P("coil", None, "slab", None),
        check_vma=False,
    )
```

```python
import functools
import math

import jax
import jax.numpy as jnp
import numpy as np
from jax import lax
from jax.experimental import pallas as pl
from jax.experimental.pallas import tpu as pltpu
from jax.sharding import PartitionSpec as P

PHASES = 8
LANES = 128
UNROLL = 8
VLIM = 52
ROWS = 16
MESH = pl.DeviceIdType.MESH


def ORDER(slab):
    return range(1, slab)


def up(value, unit):
    return -(-value // unit) * unit


def dense_table(rows, row_ok, length):
    turns = rows[:, None].astype(np.int64) * np.arange(length)[None, :] % length
    angles = turns.astype(np.float64) * (2.0 * math.pi / length)
    scaling = row_ok[:, None] / math.sqrt(length)
    cos, sin = np.cos(angles) * scaling, np.sin(angles) * scaling
    return np.concatenate([cos, sin], 1), np.concatenate([-sin, cos], 1)


def kernel(
    dims,
    kspace_ref, maps_ref, index_ref, ky_ref, kz_ref, out_ref,
    raw, index, samples, grid, maps, ky_tab, kz_tab, send, recv, image, part_send, part_recv,
    in_sem, send_sem, recv_sem, own_sem, psend_sem, precv_sem,
):
    slab, coil, coils, offs, xr, kzb, kzp, lines, ny, yb, nz = dims
    me_s, me_c = lax.axis_index("slab"), lax.axis_index("coil")
    rows = 2 * coils * slab
    kzs = up(kzb, 8)
    chunks = xr // slab
    xo = xr // coil
    owners = slab // xo
    blocks = kzp // ROWS

    barrier = pltpu.get_barrier_semaphore()
    for o in range(1, slab):
        pl.semaphore_signal(
            barrier, inc=1, device_id={"slab": lax.rem(me_s + o, slab)}, device_id_type=MESH
        )
    for o in range(1, coil):
        pl.semaphore_signal(
            barrier, inc=1, device_id={"coil": lax.rem(me_c + o, coil)}, device_id_type=MESH
        )

    def chunk_of(k):
        return lax.rem(lax.div(me_c, owners) + 1 + k, chunks)

    def load_k(k):
        at = pl.ds(chunk_of(k) * slab, slab)
        return pltpu.make_async_copy(
            kspace_ref.at[:, :, :, at], raw.at[:, :, :, at], in_sem.at[3 + k]
        )

    load_i = pltpu.make_async_copy(index_ref, index, in_sem.at[3 + chunks])
    load_i.start()
    load_k(0).start()
    load_m = pltpu.make_async_copy(maps_ref, maps, in_sem.at[0])
    load_y = pltpu.make_async_copy(ky_ref, ky_tab, in_sem.at[1])
    load_z = pltpu.make_async_copy(kz_ref, kz_tab, in_sem.at[2])
    load_y.start()
    for k in range(1, chunks):
        load_k(k).start()
    load_m.start()
    load_z.start()

    if kzp != kzb:
        grid[...] = jnp.zeros_like(grid)

    count = min(ROWS, kzb)

    def unpack(first, b, i, carry):
        kz_at = pl.multiple_of(b * ROWS, ROWS)
        for c in range(coils):
            for t in range(offs):
                angle = 2.0 * math.pi * t / PHASES
                real = raw[0, c, t, first + i, pl.ds(kz_at, count)].astype(jnp.float32)
                imag = raw[1, c, t, first + i, pl.ds(kz_at, count)].astype(jnp.float32)
                if t:
                    cosine, sine = math.cos(angle), math.sin(angle)
                    real, imag = cosine * real + sine * imag, cosine * imag - sine * real
                for part, value in ((0, real), (1, imag)):
                    at = pl.multiple_of(((part * coils + c) * slab + i) * kzs + kz_at, 8)
                    samples[t, pl.ds(at, count), :] = value
        return carry

    ky_at = lax.broadcasted_iota(jnp.int32, (ny, offs * lines), 0)

    def place(first_kz, step, carry):
        kz = first_kz + step
        picked = jnp.concatenate([index[t, pl.ds(kz, 1), :] for t in range(offs)], axis=1)
        hot = jnp.where(ky_at == picked, 1.0, 0.0).astype(jnp.bfloat16)
        left = jnp.concatenate(
            [samples[t, pl.ds(kz, rows, stride=kzs), :].astype(jnp.bfloat16) for t in range(offs)],
            axis=1,
        )
        grid_at = pl.multiple_of(kz * rows, 8)
        placed = lax.dot_general(
            left, hot, (((1,), (1,)), ((), ())), preferred_element_type=jnp.float32
        )
        for j in range(ny // LANES):
            grid[j, pl.ds(grid_at, rows), :] = placed[:, j * LANES : (j + 1) * LANES]
        return carry


    def block_copy(k, c, o, kz_at):
        return pltpu.make_async_remote_copy(
            src_ref=send.at[k, c, lax.rem(me_s + o, slab), :, pl.ds(kz_at, ROWS)],
            dst_ref=recv.at[k, c, me_s, :, pl.ds(kz_at, ROWS)],
            send_sem=send_sem.at[k, c, o],
            recv_sem=recv_sem.at[k, c, o],
            device_id={"slab": lax.rem(me_s + o, slab)},
            device_id_type=MESH,
        )

    def send_copy(k, c, o):
        return pltpu.make_async_remote_copy(
            src_ref=send.at[k, c, lax.rem(me_s + o, slab)],
            dst_ref=recv.at[k, c, me_s],
            send_sem=send_sem.at[k, c, o],
            recv_sem=recv_sem.at[k, c, o],
            device_id={"slab": lax.rem(me_s + o, slab)},
            device_id_type=MESH,
        )

    def recv_copy(k, c, o):
        return pltpu.make_async_remote_copy(
            src_ref=send.at[k, c, lax.rem(me_s + o, slab)],
            dst_ref=recv.at[k, c, lax.rem(me_s + slab - o, slab)],
            send_sem=send_sem.at[k, c, o],
            recv_sem=recv_sem.at[k, c, o],
            device_id={"slab": lax.rem(me_s + o, slab)},
            device_id_type=MESH,
        )

    def own_copy(k, c):
        return pltpu.make_async_copy(send.at[k, c, me_s], recv.at[k, c, me_s], own_sem.at[k, c])

    lane = lax.broadcasted_iota(jnp.int32, (ROWS, LANES), 1)

    def rows_pass(k, b, c, carry):
        kz_at = pl.multiple_of(b * ROWS, ROWS)
        lefts = []
        for i in range(slab):
            pieces = []
            for part in range(2):
                at = (part * coils + c) * slab + i
                for j in range(ny // LANES):
                    here = grid[j, pl.ds(kz_at * rows + at, ROWS, stride=rows), :]
                    pieces.append(here.astype(jnp.bfloat16))
            lefts.append(jnp.concatenate(pieces, axis=1))
        hybrid = jnp.dot(
            jnp.concatenate(lefts, axis=0), ky_tab[...], preferred_element_type=jnp.float32
        )
        for part in range(2):
            turned = []
            for i in range(slab):
                value = hybrid[i * ROWS : (i + 1) * ROWS, part * ny : (part + 1) * ny]
                turned.append(pltpu.roll(value, i * yb, 1) if i else value)
            for d in range(slab):
                for j in range(ny // LANES):
                    low, high = j * LANES // yb, ((j + 1) * LANES - 1) // yb
                    cut = slice(j * LANES, (j + 1) * LANES)
                    tile = turned[(low - d) % slab][:, cut]
                    for p in range(low + 1, high + 1):
                        tile = jnp.where(
                            lane >= p * yb - j * LANES, turned[(p - d) % slab][:, cut], tile
                        )
                    send[k, c, d, part, pl.ds(kz_at, ROWS), cut] = tile.astype(jnp.bfloat16)
        @pl.when((k == 0) & (b == 0) & (c == 0))
        def _():
            pl.semaphore_wait(barrier, slab + coil - 2)

        for o in ORDER(slab):
            block_copy(k, c, o, kz_at).start()

        @pl.when(b == blocks - 1)
        def _():
            own_copy(k, c).start()

        return carry

    def chunk_pass(k, carry):
        first = chunk_of(k) * slab
        load_k(k).wait()

        def block_pass(b, inner):
            lax.fori_loop(0, slab, functools.partial(unpack, first, b), 0)
            lax.fori_loop(0, count, functools.partial(place, b * ROWS), 0, unroll=UNROLL)
            return lax.fori_loop(0, coils, functools.partial(rows_pass, k, b), inner)

        return lax.fori_loop(0, blocks, block_pass, carry)

    load_i.wait()
    load_y.wait()
    lax.fori_loop(0, chunks, chunk_pass, 0)
    load_m.wait()
    load_z.wait()

    def part_copy(k, q):
        owner = chunk_of(k) * owners + q
        return pltpu.make_async_remote_copy(
            src_ref=part_send.at[chunk_of(k), pl.ds(q * xo, xo)],
            dst_ref=part_recv.at[lax.rem(owner - me_c + coil, coil)],
            send_sem=psend_sem.at[k, q],
            recv_sem=precv_sem.at[lax.rem(owner - me_c + coil, coil)],
            device_id={"coil": owner},
            device_id_type=MESH,
        )

    def depth_pass(k, carry):
        first = chunk_of(k) * slab

        def one_coil(c, inner):
            own_copy(k, c).wait()
            for o in range(1, slab):
                recv_copy(k, c, o).wait_recv()
            block = recv[k, c].reshape(slab * 2 * kzp, slab * yb)
            image[c] = lax.dot_general(
                block, kz_tab[...], (((0,), (0,)), ((), ())), preferred_element_type=jnp.float32
            )
            return inner

        lax.fori_loop(0, coils, one_coil, 0)
        for p in range(slab):
            x = lax.rem(p - me_s + slab, slab)
            add_real = add_imag = None
            for c in range(coils):
                real = image[c, p * yb : (p + 1) * yb, :nz]
                imag = image[c, p * yb : (p + 1) * yb, nz:]
                map_real = maps[0, c, first + x].astype(jnp.float32)
                map_imag = maps[1, c, first + x].astype(jnp.float32)
                term_real = map_real * real + map_imag * imag
                term_imag = map_real * imag - map_imag * real
                add_real = term_real if add_real is None else add_real + term_real
                add_imag = term_imag if add_imag is None else add_imag + term_imag
            part_send[chunk_of(k), x, 0] = add_real.astype(jnp.bfloat16)
            part_send[chunk_of(k), x, 1] = add_imag.astype(jnp.bfloat16)
        for q in range(owners):
            @pl.when(chunk_of(k) * owners + q != me_c)
            def _():
                part_copy(k, q).start()
        return carry

    lax.fori_loop(0, chunks, depth_pass, 0)

    for o in range(1, coil):
        pltpu.make_async_remote_copy(
            src_ref=part_recv.at[o],
            dst_ref=part_recv.at[o],
            send_sem=psend_sem.at[0, 0],
            recv_sem=precv_sem.at[o],
            device_id={"coil": lax.rem(me_c + o, coil)},
            device_id_type=MESH,
        ).wait_recv()
    own_chunk, own_at = lax.div(me_c, owners), lax.rem(me_c, owners) * xo

    def total(i, carry):
        value = part_send[own_chunk, own_at + i].astype(jnp.float32)
        for o in range(1, coil):
            value = value + part_recv[o, i].astype(jnp.float32)
        out_ref[i] = value
        return carry

    lax.fori_loop(0, xo, total, 0)

    def drain(k, carry):
        for c in range(coils):
            for o in range(1, slab):
                send_copy(k, c, o).wait_send()
        for q in range(owners):
            @pl.when(chunk_of(k) * owners + q != me_c)
            def _():
                part_copy(k, q).wait_send()
        return carry

    lax.fori_loop(0, chunks, drain, 0)


def local(mesh, kspace, coil_maps, line_index):
    slab, coil = mesh.shape["slab"], mesh.shape["coil"]
    _, coils, offs, xr, kzb, lines = kspace.shape
    yb, nz = coil_maps.shape[3:]
    ny = yb * slab
    kzp = up(kzb, 16)
    dims = (slab, coil, coils, offs, xr, kzb, kzp, lines, ny, yb, nz)
    chunks, xo = xr // slab, xr // coil
    owners = slab // xo
    rows = 2 * coils * slab
    f32, bf16 = jnp.float32, jnp.bfloat16

    ky_table = np.concatenate(dense_table(np.arange(ny), np.ones(ny), ny), 0)
    local_kz = np.arange(kzp)
    per_slab = []
    for s in range(slab):
        per_slab += dense_table(s * kzb + local_kz, (local_kz < kzb) * 1.0, nz)
    kz_table = np.concatenate(per_slab, 0)
    ky_table = jnp.asarray(ky_table.astype(np.float32)).astype(bf16)
    kz_table = jnp.asarray(kz_table.astype(np.float32)).astype(bf16)

    vmem, hbm = pl.BlockSpec(memory_space=pltpu.VMEM), pl.BlockSpec(memory_space=pltpu.HBM)
    dma = pltpu.SemaphoreType.DMA
    return pl.pallas_call(
        functools.partial(kernel, dims),
        out_shape=jax.ShapeDtypeStruct((xo, 2, yb, nz), f32),
        in_specs=[hbm] * 5,
        out_specs=vmem,
        scratch_shapes=[
            pltpu.VMEM(kspace.shape, bf16),
            pltpu.VMEM(line_index.shape, jnp.int32),
            pltpu.VMEM((offs, rows * up(kzb, 8), lines), f32),
            pltpu.VMEM((ny // LANES, kzp * rows, LANES), f32),
            pltpu.VMEM(coil_maps.shape, bf16),
            pltpu.VMEM(ky_table.shape, bf16),
            pltpu.VMEM(kz_table.shape, bf16),
            pltpu.VMEM((chunks, coils, slab, 2, kzp, ny), bf16),
            pltpu.VMEM((chunks, coils, slab, 2, kzp, ny), bf16),
            pltpu.VMEM((coils, ny, 2 * nz), f32),
            pltpu.VMEM((chunks, slab, 2, yb, nz), bf16),
            pltpu.VMEM((coil, xo, 2, yb, nz), bf16),
            dma((4 + chunks,)),
            dma((chunks, coils, slab)),
            dma((chunks, coils, slab)),
            dma((chunks, coils)),
            dma((chunks, owners)),
            dma((coil,)),
        ],
        compiler_params=pltpu.CompilerParams(
            collective_id=0, has_side_effects=True, vmem_limit_bytes=VLIM * 1024 * 1024
        ),
    )(kspace, coil_maps, line_index, ky_table, kz_table)


def solution(mesh):
    placed = (
        P(None, "coil", None, None, "slab", None),
        P(None, "coil", None, "slab", None),
        P(None, "slab", None),
    )
    return jax.shard_map(
        functools.partial(local, mesh),
        mesh=mesh,
        in_specs=placed,
        out_specs=P("coil", None, "slab", None),
        check_vma=False,
    )
```
